32 devices in a mesh: row: 4 (over y, x), col: 8 (over z, core).
Axes of the slice: x: 2, y: 2, z: 4, core: 2. Of those that a mesh axis runs over, the one named last changes fastest.
Arguments:
- omega: bfloat16 [16384, 16384], P('row', 'col'), may hold values from -0.36 to 2, as said below
- samples: bfloat16 [512, 16384], P(None, 'col'), may hold values from -6 to 6
- pair_tiles: int32 [320, 2], replicated, may hold values from 0 to 127, as said below
- step: float32 [1], replicated, may hold values from 0.5 to 1
- penalty: int32 [1], replicated, may hold values from 0 to 15
Outputs:
- new_upper: float32 [320, 128, 128], P(('row', 'col'))
- new_lower: float32 [320, 128, 128], P(('row', 'col'))
The draws below stay inside these ranges and needn't reach their ends.
Inputs may be any that keep to these rules, and one draw needn't show every extreme that they name: `omega`: diagonal entries lie between 1 and 2; the others are small and dense. `pair_tiles`: each row is a tile pair (I, J) with I <= J; no owner lists a pair twice, and a pair may be listed by several owners. Rows k * 10 to (k + 1) * 10 - 1 belong to owner k, counted over row+col with row the slower. Taking as a row block the tile rows held by one index of row, each owner has exactly one pair for every pair of row blocks (block of I no later than block of J). Of the distinct tiles (I, J) and (J, I) of one owner at most one lies in the block of omega held by any one device.
All inputs are finite; a program needn't handle non-finite values.
Results may differ from the reference program's by a relative error of at most 0.0058.
Values may be sent and summed in bfloat16 or wider, within the bound.
No kernel may reach another device: no remote copies, remote signals or barrier semaphores. Data moves between devices by JAX's collectives and lax.ppermute only.
A program may use at most 128 MiB of HBM per device.

```python
import math
import jax
import jax.numpy as jnp
import numpy as np
from jax import lax

P_SIZE = 16384
TILE = 128
NS = 512
PAIR_DEV = 10
N_ROW = 4
DEVICES = 32


def draw_omega(key, part):
    noise_key, diag_key = jax.random.split(key)
    values = jnp.clip(0.06 * jax.random.normal(noise_key, (P_SIZE, P_SIZE), jnp.float32), -0.36, 0.36)
    diagonal = jax.random.uniform(diag_key, (P_SIZE,), jnp.float32, 1.0, 2.0)
    positions = jnp.arange(P_SIZE)
    values = values.at[positions, positions].set(diagonal)
    return values.astype(jnp.bfloat16)


def draw_pair_tiles(key, part):
    block_tiles = P_SIZE // TILE // N_ROW
    half_tiles = block_tiles // 2
    first_blocks, second_blocks = np.triu_indices(N_ROW)
    cand_first = np.concatenate([np.repeat(np.arange(half_tiles), half_tiles), np.arange(block_tiles)])
    cand_second = np.concatenate([np.tile(np.arange(half_tiles) + half_tiles, half_tiles), np.arange(block_tiles)])
    cand_count = int(cand_first.shape[0])
    repeats = -(-DEVICES // cand_count)
    cand_first = jnp.asarray(cand_first, jnp.int32)
    cand_second = jnp.asarray(cand_second, jnp.int32)
    subkeys = jax.random.split(jax.random.fold_in(key, 7), PAIR_DEV + 1)
    upper_list = []
    lower_list = []
    for block_pair in range(PAIR_DEV):
        row_block = int(first_blocks[block_pair])
        col_block = int(second_blocks[block_pair])
        if row_block == col_block:
            order = jax.random.permutation(subkeys[block_pair], cand_count)
            chosen = jnp.tile(order, repeats)[:DEVICES]
            offset_upper = cand_first[chosen]
            offset_lower = cand_second[chosen]
        else:
            chosen = jax.random.permutation(subkeys[block_pair], block_tiles * block_tiles)[:DEVICES]
            offset_upper = chosen // block_tiles
            offset_lower = chosen % block_tiles
        upper_list.append(row_block * block_tiles + offset_upper)
        lower_list.append(col_block * block_tiles + offset_lower)
    upper_tiles = jnp.stack(upper_list, axis=1)
    lower_tiles = jnp.stack(lower_list, axis=1)
    owner_keys = jax.random.split(subkeys[PAIR_DEV], DEVICES)
    ordering = jax.vmap(lambda owner_key: jax.random.permutation(owner_key, PAIR_DEV))(owner_keys)
    upper_tiles = jnp.take_along_axis(upper_tiles, ordering, axis=1)
    lower_tiles = jnp.take_along_axis(lower_tiles, ordering, axis=1)
    return jnp.stack([upper_tiles.reshape(-1), lower_tiles.reshape(-1)], axis=1).astype(jnp.int32)


def levels(own_key, extent, shards, least, largest):
    gain, own = 1.0, jax.random.fold_in(own_key, 6)
    for position, shards_of in shards:
        draws = jnp.exp(jax.random.uniform(jax.random.fold_in(own, position), (shards_of,), jnp.float32, least / len(shards), largest / len(shards)))
        gain = gain * jnp.repeat(draws, extent[position] // shards_of).reshape([-1 if axis == position else 1 for axis in range(len(extent))])
    return gain


def gaussian(rng, shape, width, reach, pieces=(), held_as=jnp.bfloat16):
    array = jax.random.normal(rng, shape, jnp.float32) * width
    if len(pieces) > 0:
        array = levels(rng, shape, pieces, -0.22, 0.18) * array
    return jnp.clip(array, min=-reach, max=reach).astype(held_as)


def setup_inputs(seed: int = 0) -> dict:
    key_list = jax.random.split(jax.random.key(seed), 6)
    omega = draw_omega(jax.random.fold_in(key_list[5], 71), 0)
    samples = gaussian(key_list[1], (NS, P_SIZE), 1.0, 6.0, ((1, 8),))
    pair_tiles = draw_pair_tiles(jax.random.fold_in(key_list[5], 71), 0)
    step = jnp.clip(jnp.exp(jax.random.uniform(key_list[3], (1,), jnp.float32, math.log(0.5), math.log(1.0))), 0.5, 1.0)
    penalty = jax.random.randint(key_list[4], (1,), 0, 16).astype(jnp.int32)
    return dict(omega=omega, samples=samples, pair_tiles=pair_tiles, step=step, penalty=penalty)


def reference(omega, samples, pair_tiles, step, penalty):
    projected = jnp.dot(omega, samples.T, preferred_element_type=jnp.float32).astype(jnp.bfloat16)
    identity = jnp.eye(TILE, dtype=jnp.float32)
    scale = step[0]
    weight = 0.3 * jnp.exp(-0.12 * penalty[0].astype(jnp.float32))

    def one_pair(pair):
        upper_start = pair[0].astype(jnp.int32) * TILE
        lower_start = pair[1].astype(jnp.int32) * TILE
        rows_upper = lax.dynamic_slice_in_dim(projected, upper_start, TILE, 0)
        rows_lower = lax.dynamic_slice_in_dim(projected, lower_start, TILE, 0)
        cols_upper = lax.dynamic_slice_in_dim(samples, upper_start, TILE, 1)
        cols_lower = lax.dynamic_slice_in_dim(samples, lower_start, TILE, 1)
        forward = jnp.dot(rows_upper, cols_lower, preferred_element_type=jnp.float32) / NS
        backward = jnp.dot(rows_lower, cols_upper, preferred_element_type=jnp.float32) / NS
        forward = lax.optimization_barrier(forward.astype(jnp.bfloat16)).astype(jnp.float32)
        backward = lax.optimization_barrier(backward.astype(jnp.bfloat16)).astype(jnp.float32)
        gradient = (forward + backward.T) * 0.5
        omega_upper = lax.dynamic_slice(omega, (upper_start, lower_start), (TILE, TILE)).astype(jnp.float32)
        omega_lower = lax.dynamic_slice(omega, (lower_start, upper_start), (TILE, TILE)).astype(jnp.float32)
        on_diagonal = (pair[0] == pair[1]).astype(jnp.float32)
        diag_mask = identity * on_diagonal
        diag_values = jnp.sum(omega_upper * identity, axis=1)
        inverse = 1.0 / jnp.where(on_diagonal > 0, diag_values, 1.0)
        gradient = gradient - diag_mask * inverse[:, None]
        bound = scale * weight * (1.0 - diag_mask)
        upper_value = omega_upper - scale * gradient
        lower_value = omega_lower - scale * gradient.T
        new_upper = upper_value - jnp.clip(upper_value, -bound, bound)
        new_lower = lower_value - jnp.clip(lower_value, -bound, bound)
        return new_upper, new_lower

    new_upper, new_lower = lax.map(one_pair, pair_tiles)
    return new_upper, new_lower
```

```python
import functools

import jax
import jax.numpy as jnp
from jax import lax
from jax.experimental import pallas as pl
from jax.experimental.pallas import tpu as pltpu
from jax.sharding import Mesh, PartitionSpec as P

TILE = 128
ANY = pl.BlockSpec(memory_space=pl.ANY)
SMEM = pl.BlockSpec(memory_space=pltpu.SMEM)
VMEM = pl.BlockSpec(memory_space=pltpu.VMEM)
AXES = ("row", "chip", "core")


def tile_at(index):
    return pl.ds(pl.multiple_of(index * TILE, TILE), TILE)


def pick_kernel(rows, cols, omega, out, sems):
    count = out.shape[0]

    def copy(i):
        return pltpu.make_async_copy(
            omega.at[tile_at(rows[i]), tile_at(cols[i])], out.at[i], sems.at[i]
        )

    def start(i, carry):
        copy(i).start()
        return carry

    def wait(i, carry):
        copy(i).wait()
        return carry

    lax.fori_loop(0, count, start, 0)
    lax.fori_loop(0, count, wait, 0)


def pick_tiles(omega, rows, cols):
    count = rows.shape[0]
    return pl.pallas_call(
        pick_kernel,
        out_shape=jax.ShapeDtypeStruct((count, TILE, TILE), omega.dtype),
        in_specs=[SMEM, SMEM, ANY],
        out_specs=VMEM,
        scratch_shapes=[pltpu.SemaphoreType.DMA((count,))],
        name="pick_tiles",
    )(rows, cols, omega)


def moment_kernel(samples_scale, rows, cols, info, shared, own, other, out):
    count = out.shape[0]
    core, diagonal = info[0], info[1]
    half = own.shape[1] // TILE

    def product(row, col, write):
        def from_block(block):
            value = jnp.dot(
                shared[tile_at(row), :],
                block[:, tile_at(lax.rem(col, half))],
                preferred_element_type=jnp.float32,
            )
            write((value * samples_scale).astype(jnp.bfloat16))

        pl.when(col // half == core)(lambda: from_block(own))
        pl.when(col // half != core)(lambda: from_block(other))

    def step(i, carry):
        def write(value):
            out[i] = value

        product(rows[i], cols[i], write)
        return carry

    def merge(i, carry):
        def write(value):
            partner = value.astype(jnp.float32).T
            out[i] = ((out[i].astype(jnp.float32) + partner) * 0.5).astype(jnp.bfloat16)

        product(cols[i], rows[i], write)
        return carry

    lax.fori_loop(0, count, step, 0)

    @pl.when(diagonal == 1)
    def _():
        lax.fori_loop(0, count, merge, 0)


def moment_tiles(shared, own, other, rows, cols, info):
    count = rows.shape[0]
    depth = shared.shape[1]
    return pl.pallas_call(
        functools.partial(moment_kernel, 1.0 / depth),
        out_shape=jax.ShapeDtypeStruct((count, TILE, TILE), jnp.bfloat16),
        in_specs=[SMEM, SMEM, SMEM, VMEM, VMEM, VMEM],
        out_specs=VMEM,
        compiler_params=pltpu.CompilerParams(vmem_limit_bytes=32 * 1024 * 1024),
        name="moment_tiles",
    )(rows, cols, info, shared, own, other)


def update_kernel(
    table, scalars, mine_up, mine_low, omega_up, omega_low, new_upper, new_lower
):
    k = pl.program_id(0)
    merged, equal = table[4, k], table[5, k]
    scale, weight = scalars[0], scalars[1]
    up = mine_up[0].astype(jnp.float32)
    low = mine_low[0].astype(jnp.float32).T
    gradient = jnp.where(merged == 1, up, (up + low) * 0.5)
    upper = omega_up[0].astype(jnp.float32)
    lower = omega_low[0].astype(jnp.float32)
    row = lax.broadcasted_iota(jnp.int32, (TILE, TILE), 0)
    col = lax.broadcasted_iota(jnp.int32, (TILE, TILE), 1)
    diagonal = (row == col) & (equal == 1)
    gradient = gradient - jnp.where(diagonal, 1.0 / jnp.where(diagonal, upper, 1.0), 0.0)
    bound = jnp.where(diagonal, 0.0, scale * weight)
    upper_value = upper - scale * gradient
    lower_value = lower - scale * gradient.T
    new_upper[0] = upper_value - jnp.clip(upper_value, -bound, bound)
    new_lower[0] = lower_value - jnp.clip(lower_value, -bound, bound)


def update(got_moments, got_omega, table, scalars):
    count = table.shape[1]
    tile = (1, TILE, TILE)

    def slot(line):
        return pl.BlockSpec(tile, lambda k, table, scalars: (table[line, k], 0, 0))

    out = pl.BlockSpec(tile, lambda k, table, scalars: (k, 0, 0))
    shape = jax.ShapeDtypeStruct((count, TILE, TILE), jnp.float32)
    return pl.pallas_call(
        update_kernel,
        out_shape=(shape, shape),
        grid_spec=pltpu.PrefetchScalarGridSpec(
            num_scalar_prefetch=2,
            grid=(count,),
            in_specs=[slot(0), slot(1), slot(2), slot(3)],
            out_specs=[out, out],
        ),
        name="update",
    )(table, scalars, got_moments, got_moments, got_omega, got_omega)


def local(omega, samples, pair_tiles, step, penalty):
    rows, chips, cores = (lax.axis_size(name) for name in AXES)
    row, chip, core = (lax.axis_index(name) for name in AXES)
    own_index = (row * chips + chip) * cores + core
    row_tiles = omega.shape[0] // TILE
    col_tiles = omega.shape[1] // TILE
    devices = rows * chips * cores
    pair_count = pair_tiles.shape[0] // devices
    other = lax.ppermute(samples, "core", [(i, cores - 1 - i) for i in range(cores)])

    pairs = pair_tiles.reshape(devices, pair_count, 2)
    first, second = pairs[:, :, 0], pairs[:, :, 1]
    wanted = (first // row_tiles == jnp.minimum(row, chip)) & (
        second // row_tiles == jnp.maximum(row, chip)
    )
    wanted = wanted.astype(jnp.int32)
    upper = jnp.sum(wanted * first, axis=1)
    lower = jnp.sum(wanted * second, axis=1)
    flip = row > chip
    tile_row = jnp.where(flip, lower, upper) - row * row_tiles
    tile_col = jnp.where(flip, upper, lower) - chip * row_tiles
    mine = lambda x: lax.dynamic_index_in_dim(
        x.reshape(rows * chips, cores), core, 1, keepdims=False
    )
    held = tile_col // col_tiles == core
    use_swapped = (row == chip) & ~held
    omega_row = jnp.where(use_swapped, tile_col, tile_row)
    omega_col = jnp.where(use_swapped, tile_row, tile_col) % col_tiles
    sent_omega = pick_tiles(omega, omega_row, omega_col)
    got_omega = lax.all_to_all(sent_omega, AXES, split_axis=0, concat_axis=0, tiled=True)

    partial_value = lax.dot_general(
        omega, samples, (((1,), (1,)), ((), ())), preferred_element_type=jnp.float32
    )
    scattered = lax.psum_scatter(
        partial_value, ("chip", "core"), scatter_dimension=0, tiled=True
    ).astype(jnp.bfloat16)
    shared = lax.all_gather(scattered, ("chip", "core"), axis=0, tiled=True)
    info = jnp.stack([core, (row == chip).astype(jnp.int32)])
    sent_moments = moment_tiles(
        shared,
        samples,
        other,
        mine(tile_row),
        mine(tile_col),
        info,
    )
    got_moments = lax.all_to_all(
        sent_moments, ("row", "chip"), split_axis=0, concat_axis=0, tiled=True
    )

    mine_pairs = lax.dynamic_index_in_dim(pairs, own_index, 0, keepdims=False)
    one, two = mine_pairs[:, 0], mine_pairs[:, 1]
    one_block, two_block = one // row_tiles, two // row_tiles
    table = jnp.stack(
        [
            one_block * chips + two_block,
            two_block * chips + one_block,
            one_block * chips * cores + two // col_tiles,
            two_block * chips * cores + one // col_tiles,
            (one_block == two_block).astype(jnp.int32),
            (one == two).astype(jnp.int32),
        ]
    )
    weight = 0.3 * jnp.exp(-0.12 * penalty.astype(jnp.float32))
    scalars = jnp.concatenate([step, weight])
    return update(got_moments, got_omega, table, scalars)


def solution(mesh):
    rows, cols = mesh.shape["row"], mesh.shape["col"]
    cores = cols // rows
    view = Mesh(mesh.devices.reshape(rows, rows, cores), AXES)
    placed = (P("row", ("chip", "core")), P(None, ("chip", "core")), P(), P(), P())
    out = P(AXES, None, None)
    return jax.shard_map(
        local, mesh=view, in_specs=placed, out_specs=(out, out), check_vma=False
    )
```
